256 devices in a mesh: dp: 16 (over z_hi, x, core), fsdp: 16 (over z_lo, y).
Axes of the slice: x: 4, y: 4, z: 8 (z_hi: 2, z_lo: 4; z = z_hi * 4 + z_lo), core: 2. Of those that a mesh axis runs over, the one named last changes fastest.
Arguments:
- attn_heads: bfloat16 [512, 4096], P('dp', 'fsdp'), may hold values from -6 to 6
- out_proj: bfloat16 [4096, 4608], P('fsdp'), may hold values from -0.09375 to 0.09375
- resid_pre: bfloat16 [512, 4608], P(('dp', 'fsdp')), may hold values from -25 to 25
- post_gain: float32 [4608], replicated, may hold values from 0.5 to 1.5
- enc_weight: bfloat16 [4608, 65536], P(None, ('dp', 'fsdp')), may hold values from -0.09375 to 0.09375
- enc_bias: float32 [65536], P(('dp', 'fsdp')), may hold values from -3 to 3
- dec_weight: bfloat16 [65536, 4608], P(('dp', 'fsdp')), may hold values from -0.046875 to 0.046875
- dec_bias: float32 [4608], replicated, may hold values from -3 to 3
Outputs:
- enc_grad: bfloat16 [4608, 65536], P(None, ('dp', 'fsdp'))
- enc_bias_grad: float32 [65536], P(('dp', 'fsdp'))
- dec_grad: bfloat16 [65536, 4608], P(('dp', 'fsdp'))
- dec_bias_grad: float32 [4608], replicated
- loss: float32 [], replicated
The draws below stay inside these ranges and needn't reach their ends.
All inputs are finite; a program needn't handle non-finite values.
Results may differ from the reference program's by a relative error of at most 0.013.
Values may be sent and summed in bfloat16 or wider, within the bound.
A program may use at most 128 MiB of HBM per device.

```python
import jax
import jax.numpy as jnp
from jax import lax

D = 4608
LAT = 65536
TOKENS = 512
ATTN = 4096


def draw_resid_pre(key, part):
    first, second = jax.random.split(key, 2)
    place = jnp.arange(TOKENS, dtype=jnp.float32) / max(TOKENS - 1, 1)
    rough = jnp.exp(jax.random.uniform(first, (TOKENS,), minval=-0.7, maxval=0.7))
    scale = (0.5 + 2.5 * place) * rough
    entries = jnp.clip(jax.random.normal(second, (TOKENS, D)), -4.0, 4.0)
    return jnp.clip(scale[:, None] * entries, -25.0, 25.0).astype(jnp.bfloat16)


def draw_dec_weight(key, part):
    first, second = jax.random.split(key, 2)
    place = jnp.arange(LAT, dtype=jnp.float32) / (LAT - 1)
    rough = jnp.exp(jax.random.uniform(first, (LAT,), minval=-0.7, maxval=0.7))
    scale = (0.5 + place) * rough
    entries = jnp.clip(jax.random.normal(second, (LAT, D)), -4.0, 4.0)
    limit = 12.0 * LAT ** (-0.5)
    return jnp.clip(scale[:, None] * entries * LAT ** (-0.5), -limit, limit).astype(jnp.bfloat16)


def steps_of(key, shape, cuts, low, top_value):
    gain, own = 1.0, jax.random.fold_in(key, 6)
    for dim, blocks in cuts:
        heights = jnp.exp(jax.random.uniform(jax.random.fold_in(own, dim), (blocks,), jnp.float32, low / len(cuts), top_value / len(cuts)))
        gain = gain * jnp.repeat(heights, shape[dim] // blocks).reshape([-1 if axis == dim else 1 for axis in range(len(shape))])
    return gain


def noise(key, shape, deviation, most, shards=(), kind=jnp.bfloat16):
    factor_of = steps_of(key, shape, shards, -0.22, 0.18) if shards else 1.0
    array = jax.random.normal(key, shape, jnp.float32) * deviation * factor_of
    return jnp.minimum(jnp.maximum(array, -most), most).astype(kind)


def setup_inputs(seed: int = 0) -> dict:
    arg_keys = jax.random.split(jax.random.key(seed), 9)
    attn_heads = noise(arg_keys[0], (TOKENS, ATTN), 1.0, 6.0, ((0, 16), (1, 16)))
    out_proj = noise(arg_keys[1], (ATTN, D), ATTN ** -0.5, 0.09375, ((0, 16),))
    resid_pre = draw_resid_pre(jax.random.fold_in(arg_keys[8], 71), 0)
    post_gain = jnp.clip(1.0 + 0.1 * jax.random.normal(arg_keys[3], (D,), jnp.float32), 0.5, 1.5)
    enc_weight = noise(arg_keys[4], (D, LAT), D ** -0.5, 0.09375, ((1, 256),))
    enc_bias = noise(arg_keys[5], (LAT,), 0.5, 3.0, ((0, 256),), jnp.float32)
    dec_weight = draw_dec_weight(jax.random.fold_in(arg_keys[8], 71), 0)
    dec_bias = noise(arg_keys[7], (D,), 0.5, 3.0, (), jnp.float32)
    return dict(attn_heads=attn_heads, out_proj=out_proj, resid_pre=resid_pre, post_gain=post_gain, enc_weight=enc_weight, enc_bias=enc_bias, dec_weight=dec_weight, dec_bias=dec_bias)


SPARSITY = 0.25
SMOOTHING = 0.1
EPSILON = 1e-06

def reference(attn_heads, out_proj, resid_pre, post_gain, enc_weight, enc_bias, dec_weight, dec_bias):
    projected = jnp.dot(attn_heads, out_proj, preferred_element_type=jnp.float32)
    scale = lax.rsqrt(lax.optimization_barrier(jnp.mean(projected * projected, axis=-1, keepdims=True)) + EPSILON)
    residual = (resid_pre.astype(jnp.float32) + projected * scale * post_gain).astype(jnp.bfloat16)
    preact = jnp.dot(residual, enc_weight, preferred_element_type=jnp.float32) + enc_bias
    latents = jnp.maximum(preact, 0.0)
    latents_b = latents.astype(jnp.bfloat16)
    dec_f = dec_weight.astype(jnp.float32)
    row_norms = jnp.sqrt(lax.optimization_barrier(jnp.sum(dec_f * dec_f, axis=1)) + EPSILON)
    recon = jnp.dot(latents_b, dec_weight, preferred_element_type=jnp.float32) + dec_bias
    error = recon - residual.astype(jnp.float32)
    error_sum = jnp.sum(error * error)
    penalty_sum = jnp.sum(latents * row_norms)
    loss = (0.5 * error_sum + SPARSITY * penalty_sum) / (residual.shape[0] * residual.shape[1])
    error_b = error.astype(jnp.bfloat16)
    dec_bias_grad = lax.optimization_barrier(jnp.sum(error_b.astype(jnp.float32), axis=0))
    usage = lax.optimization_barrier(jnp.sum(latents, axis=0))
    dec_grad = jnp.dot(latents_b.T, error_b, preferred_element_type=jnp.float32)
    dec_grad = (dec_grad + SPARSITY * (usage / row_norms)[:, None] * dec_f).astype(jnp.bfloat16)
    latent_grad = jnp.dot(error_b, dec_weight.T, preferred_element_type=jnp.float32) + SPARSITY * row_norms
    preact_grad = latent_grad * jax.nn.sigmoid(preact / SMOOTHING)
    enc_bias_grad = lax.optimization_barrier(jnp.sum(preact_grad, axis=0))
    enc_grad = jnp.dot(residual.T, preact_grad.astype(jnp.bfloat16), preferred_element_type=jnp.float32).astype(jnp.bfloat16)
    return (enc_grad, enc_bias_grad, dec_grad, dec_bias_grad, loss)
```

```python
import jax
import jax.numpy as jnp
from jax import lax
from jax.experimental import pallas as pl
from jax.experimental.pallas import tpu as pltpu
from jax.sharding import PartitionSpec as P

SPARSITY = 0.25
SMOOTHING = 0.1
EPSILON = 1e-06

D = 4608
BLOCKS = 64
MESH = pl.DeviceIdType.MESH


def coords():
    dp, fs = lax.axis_index("dp"), lax.axis_index("fsdp")
    x = lax.rem(lax.div(dp, 2), 4)
    y = lax.rem(fs, 4)
    z = lax.div(dp, 8) * 4 + lax.div(fs, 4)
    return x, y, z, lax.rem(dp, 2)


def device(x, y, z, c):
    return ((lax.div(z, 4) * 4 + x) * 2 + c, lax.rem(z, 4) * 4 + y)


class Wire:
    def __init__(self, send_sems, recv_sems):
        self.send_sems, self.recv_sems, self.copies = send_sems, recv_sems, []

    def send(self, src, dst, target):
        n = len(self.copies)
        copy = pltpu.make_async_remote_copy(
            src_ref=src,
            dst_ref=dst,
            send_sem=self.send_sems.at[n],
            recv_sem=self.recv_sems.at[n],
            device_id=target,
            device_id_type=MESH,
        )
        copy.start()
        self.copies.append(copy)
        return copy

    def finish(self):
        for copy in self.copies:
            copy.wait_send()


def arrived(copies):
    for copy in copies:
        copy.wait_recv()


def cols(start, size):
    return pl.ds(pl.multiple_of(start, 128), size)


def greet(targets):
    barrier = pltpu.get_barrier_semaphore()
    for target in targets:
        pl.semaphore_signal(barrier, inc=1, device_id=target, device_id_type=MESH)
    pl.semaphore_wait(barrier, len(targets))


A1 = 2048
Q1 = (D - A1) // 4
W1 = D // 4


def residual_kernel(part, pre, gain, out, rs, rp, rows, full, send_sems, recv_sems):
    x, y, z, c = coords()
    zh, zl = lax.div(z, 4) * 4, lax.rem(z, 4)
    at_x = lambda d: device(lax.rem(x + d, 4), y, z, c)
    at_y = lambda d: device(x, lax.rem(y + d, 4), z, c)
    at_z = lambda d: device(x, y, lax.rem(z + d, 8), c)
    sibling = device(x, y, z, 1 - c)
    plane = {
        (a, b): device(x, lax.rem(y + a, 4), zh + lax.rem(zl + b, 4), c)
        for a in range(4)
        for b in range(4)
        if (a, b) != (0, 0)
    }
    beyond = [device(x, y, lax.rem(zl + d, 4) + 4 - zh, c) for d in range(4)]
    greet(
        list(plane.values())
        + beyond
        + [at_x(d) for d in (1, 2, 3)]
        + [sibling]
    )
    wire = Wire(send_sems, recv_sems)

    got = []
    for i, ((a, b), target) in enumerate(plane.items()):
        src = part.at[lax.rem(zl + b, 4), :, cols(lax.rem(y + a, 4) * W1, W1)]
        got.append(wire.send(src, rs.at[i], target))
    rp[y] = pre[...]
    got_pre = [wire.send(rp.at[y], rp.at[y], at_y(d)) for d in (1, 2, 3)]
    total = part[zl, :, cols(y * W1, W1)].astype(jnp.float32)
    arrived(got)
    for i in range(15):
        total = total + rs[i].astype(jnp.float32)
    full[y] = total
    got = [wire.send(full.at[y], full.at[y], at_y(d)) for d in (1, 2, 3)]
    arrived(got_pre)
    for i in range(4):
        rows[2 * i : 2 * i + 2, :] = rp[i].astype(jnp.float32)
    arrived(got)
    square = jnp.zeros((8, 1), jnp.float32)
    for i in range(4):
        square = square + jnp.sum(full[i] * full[i], axis=1, keepdims=True)
    scale = lax.rsqrt(square / D + EPSILON)
    mine = c * 32 + x * 8 + z
    for i in range(4):
        w = slice(i * W1, (i + 1) * W1)
        rows[:, w] = rows[:, w] + full[i] * scale * gain[:, w]

    a_cols, q_cols = pl.ds(0, A1), cols(A1 + y * Q1, Q1)
    out[mine, :, a_cols] = rows[:, a_cols].astype(jnp.bfloat16)
    out[mine, :, q_cols] = rows[:, q_cols].astype(jnp.bfloat16)
    half = pl.ds(c * 32, 32)
    run = pl.ds(c * 32 + x * 8, 8)
    block_a, block_q = out.at[mine, :, a_cols], out.at[mine, :, q_cols]
    got_a = [wire.send(block_a, block_a, at_z(d)) for d in range(1, 8)]
    got_q = [wire.send(block_q, block_q, at_z(d)) for d in range(1, 8)]
    arrived(got_q)
    run_q = out.at[run, :, q_cols]
    got_q = [wire.send(run_q, run_q, at_x(d)) for d in (1, 2, 3)]
    arrived(got_a)
    run_a = out.at[run, :, a_cols]
    got_a = [wire.send(run_a, run_a, at_x(d)) for d in (1, 2, 3)]
    passed = [wire.send(run_a, run_a, sibling)]
    arrived(got_q)
    half_q = out.at[half, :, q_cols]
    got_q = [wire.send(half_q, half_q, at_y(d)) for d in (1, 2, 3)]
    passed.append(wire.send(half_q, half_q, sibling))
    for d in (1, 2, 3):
        got_a[d - 1].wait_recv()
        there = out.at[pl.ds(c * 32 + lax.rem(x + 4 - d, 4) * 8, 8), :, a_cols]
        passed.append(wire.send(there, there, sibling))
    for d in (1, 2, 3):
        got_q[d - 1].wait_recv()
        there = out.at[half, :, cols(A1 + lax.rem(y + 4 - d, 4) * Q1, Q1)]
        passed.append(wire.send(there, there, sibling))
    arrived(passed)
    wire.finish()


def gather_residual(part, pre, gain):
    copies = 15 + 3 + 3 + 14 + 9 + 8
    vmem = pl.BlockSpec(memory_space=pltpu.VMEM)
    return pl.pallas_call(
        residual_kernel,
        out_shape=jax.ShapeDtypeStruct((BLOCKS, 8, D), jnp.bfloat16),
        in_specs=[vmem] * 3,
        out_specs=vmem,
        scratch_shapes=[
            pltpu.VMEM((15, 8, W1), jnp.bfloat16),
            pltpu.VMEM((4, 2, D), jnp.bfloat16),
            pltpu.VMEM((8, D), jnp.float32),
            pltpu.VMEM((4, 8, W1), jnp.float32),
            pltpu.SemaphoreType.DMA((copies,)),
            pltpu.SemaphoreType.DMA((copies,)),
        ],
        compiler_params=pltpu.CompilerParams(
            collective_id=0, has_side_effects=True, vmem_limit_bytes=24 * 2**20
        ),
        name="gather_residual",
    )(part, pre, gain)


A2 = 2560
QA = A2 // 4
C2 = D - A2
QC = C2 // 4


def error_kernel(
    part, resid, bias, penalty, out, stats,
    sib, both, ra1, rc1, acc_a, acc_c, ra2, rc2, acc_a2, acc_c2, ra3, rc3, st_z, st_x, st_y, st_c,
    send_sems, recv_sems,
):
    x, y, z, c = coords()
    at_x = lambda d: device(lax.rem(x + d, 4), y, z, c)
    at_y = lambda d: device(x, lax.rem(y + d, 4), z, c)
    at_z = lambda d: device(x, y, lax.rem(z + d, 8), c)
    sibling = device(x, y, z, 1 - c)
    greet(
        [at_x(d) for d in (1, 2, 3)]
        + [at_y(d) for d in (1, 2, 3)]
        + [at_z(d) for d in range(1, 8)]
        + [sibling]
    )
    wire = Wire(send_sems, recv_sems)
    f32 = jnp.float32
    base = c * 32
    c_cols = pl.ds(A2, C2)

    order_a = (1, 2, 3, 0)
    got_a, got_c = {}, {}
    for d in order_a:
        w = cols(lax.rem(y + d, 4) * QA, QA)
        got_a[d] = wire.send(part.at[pl.ds(32 - base, 32), :, w], sib.at[:, :, w], sibling)
        r = lax.rem(x + d, 4) * 8
        got_c[d] = wire.send(
            part.at[pl.ds(32 - base + r, 8), :, c_cols], sib.at[pl.ds(r, 8), :, c_cols], sibling
        )
    from_a, from_c = {}, {}
    for d in order_a:
        w = cols(lax.rem(y + d, 4) * QA, QA)
        got_a[d].wait_recv()

        @pl.loop(0, 32)
        def _(i):
            both[i, :, w] = (part[base + i, :, w].astype(f32) + sib[i, :, w].astype(f32)).astype(jnp.bfloat16)

        if d:
            from_a[d] = wire.send(both.at[:, :, w], ra1.at[d - 1], at_y(d))
        r = lax.rem(x + d, 4) * 8
        got_c[d].wait_recv()

        @pl.loop(0, 8)
        def _(i):
            both[r + i, :, c_cols] = (
                part[base + r + i, :, c_cols].astype(f32) + sib[r + i, :, c_cols].astype(f32)
            ).astype(jnp.bfloat16)

        if d:
            from_c[d] = wire.send(both.at[pl.ds(r, 8), :, c_cols], rc1.at[d - 1], at_x(d))

    wa, wc = cols(y * QA, QA), cols(A2 + y * QC, QC)
    arrived(from_a.values())

    @pl.loop(0, 32)
    def _(i):
        acc_a[i] = (
            both[i, :, wa].astype(f32) + ra1[0, i].astype(f32) + ra1[1, i].astype(f32) + ra1[2, i].astype(f32)
        ).astype(jnp.bfloat16)

    from_a = [
        wire.send(acc_a.at[pl.ds(lax.rem(x + d, 4) * 8, 8)], ra2.at[d - 1], at_x(d)) for d in (1, 2, 3)
    ]
    arrived(from_c.values())

    @pl.loop(0, 8)
    def _(i):
        acc_c[i] = (
            both[x * 8 + i, :, c_cols].astype(f32)
            + rc1[0, i].astype(f32) + rc1[1, i].astype(f32) + rc1[2, i].astype(f32)
        ).astype(jnp.bfloat16)

    from_c = [
        wire.send(acc_c.at[:, :, cols(lax.rem(y + d, 4) * QC, QC)], rc2.at[d - 1], at_y(d))
        for d in (1, 2, 3)
    ]

    arrived(from_a)

    @pl.loop(0, 8)
    def _(i):
        acc_a2[i] = (
            acc_a[x * 8 + i].astype(f32) + ra2[0, i].astype(f32) + ra2[1, i].astype(f32) + ra2[2, i].astype(f32)
        ).astype(jnp.bfloat16)

    from_a = [wire.send(acc_a2.at[lax.rem(z + d, 8)], ra3.at[d - 1], at_z(d)) for d in range(1, 8)]
    arrived(from_c)

    @pl.loop(0, 8)
    def _(i):
        acc_c2[i] = (
            acc_c[i, :, cols(y * QC, QC)].astype(f32)
            + rc2[0, i].astype(f32) + rc2[1, i].astype(f32) + rc2[2, i].astype(f32)
        ).astype(jnp.bfloat16)

    from_c = [wire.send(acc_c2.at[lax.rem(z + d, 8)], rc3.at[d - 1], at_z(d)) for d in range(1, 8)]

    mine = base + x * 8 + z
    square = penalty[...]

    def error_of(total, w, size, square):
        error = total + bias[:, w] - resid[mine, :, w].astype(f32)
        out[mine, :, w] = error.astype(jnp.bfloat16)
        for i in range(size // 128):
            piece = error[:, i * 128 : (i + 1) * 128]
            square = square + 0.5 * piece * piece
        return square

    arrived(from_a)
    total = acc_a2[z].astype(f32)
    for i in range(7):
        total = total + ra3[i].astype(f32)
    square = error_of(total, wa, QA, square)
    block_a = out.at[mine, :, wa]
    got_a = [wire.send(block_a, block_a, at_z(d)) for d in range(1, 8)]
    arrived(from_c)
    total = acc_c2[z].astype(f32)
    for i in range(7):
        total = total + rc3[i].astype(f32)
    square = error_of(total, wc, QC, square)
    block_c = out.at[mine, :, wc]
    got_c = [wire.send(block_c, block_c, at_z(d)) for d in range(1, 8)]
    st_z[z] = square
    got_s = [wire.send(st_z.at[z], st_z.at[z], at_z(d)) for d in range(1, 8)]

    half = pl.ds(base, 32)
    run = pl.ds(base + x * 8, 8)
    arrived(got_a)
    run_a = out.at[run, :, wa]
    got_a = [wire.send(run_a, run_a, at_x(d)) for d in (1, 2, 3)]
    arrived(got_c)
    run_c = out.at[run, :, wc]
    got_c = [wire.send(run_c, run_c, at_y(d)) for d in (1, 2, 3)]
    arrived(got_s)
    st_x[x] = sum_of(st_z, 8)
    got_s = [wire.send(st_x.at[x], st_x.at[x], at_x(d)) for d in (1, 2, 3)]
    arrived(got_a)
    half_a = out.at[half, :, wa]
    got_a = [wire.send(half_a, half_a, at_y(d)) for d in (1, 2, 3)]
    passed = [wire.send(half_a, half_a, sibling)]
    arrived(got_c)
    run_c = out.at[run, :, c_cols]
    got_c = [wire.send(run_c, run_c, at_x(d)) for d in (1, 2, 3)]
    passed.append(wire.send(run_c, run_c, sibling))
    arrived(got_s)
    st_y[y] = sum_of(st_x, 4)
    got_s = [wire.send(st_y.at[y], st_y.at[y], at_y(d)) for d in (1, 2, 3)]
    arrived(got_s)
    st_c[c] = sum_of(st_y, 4)
    got_s = wire.send(st_c.at[c], st_c.at[c], sibling)
    for d in (1, 2, 3):
        got_a[d - 1].wait_recv()
        there = out.at[half, :, cols(lax.rem(y + 4 - d, 4) * QA, QA)]
        passed.append(wire.send(there, there, sibling))
        got_c[d - 1].wait_recv()
        there = out.at[pl.ds(base + lax.rem(x + 4 - d, 4) * 8, 8), :, c_cols]
        passed.append(wire.send(there, there, sibling))
    got_s.wait_recv()
    stats[...] = st_c[0] + st_c[1]
    arrived(passed)
    wire.finish()


def sum_of(ref, n):
    total = ref[0]
    for i in range(1, n):
        total = total + ref[i]
    return total


def exchange_error(part, resid, bias, penalty):
    copies = 8 + 6 + 6 + 14 + 14 + 7 + 6 + 3 + 6 + 3 + 1 + 8
    vmem = pl.BlockSpec(memory_space=pltpu.VMEM)
    bf16 = jnp.bfloat16
    return pl.pallas_call(
        error_kernel,
        out_shape=(
            jax.ShapeDtypeStruct((BLOCKS, 8, D), bf16),
            jax.ShapeDtypeStruct((8, 128), jnp.float32),
        ),
        in_specs=[vmem] * 4,
        out_specs=(vmem, vmem),
        scratch_shapes=[
            pltpu.VMEM((32, 8, D), bf16),
            pltpu.VMEM((32, 8, D), bf16),
            pltpu.VMEM((3, 32, 8, QA), bf16),
            pltpu.VMEM((3, 8, 8, C2), bf16),
            pltpu.VMEM((32, 8, QA), bf16),
            pltpu.VMEM((8, 8, C2), bf16),
            pltpu.VMEM((3, 8, 8, QA), bf16),
            pltpu.VMEM((3, 8, 8, QC), bf16),
            pltpu.VMEM((8, 8, QA), bf16),
            pltpu.VMEM((8, 8, QC), bf16),
            pltpu.VMEM((7, 8, QA), bf16),
            pltpu.VMEM((7, 8, QC), bf16),
            pltpu.VMEM((8, 8, 128), jnp.float32),
            pltpu.VMEM((4, 8, 128), jnp.float32),
            pltpu.VMEM((4, 8, 128), jnp.float32),
            pltpu.VMEM((2, 8, 128), jnp.float32),
            pltpu.SemaphoreType.DMA((copies,)),
            pltpu.SemaphoreType.DMA((copies,)),
        ],
        compiler_params=pltpu.CompilerParams(
            collective_id=1, has_side_effects=True, vmem_limit_bytes=40 * 2**20
        ),
        name="exchange_error",
    )(part, resid, bias, penalty)


def body(attn_heads, out_proj, resid_pre, post_gain, enc_weight, enc_bias, dec_weight, dec_bias):
    f32, bf16 = jnp.float32, jnp.bfloat16
    part = jnp.dot(attn_heads, out_proj, preferred_element_type=f32).astype(bf16)
    resid = gather_residual(part.reshape(4, 8, D), resid_pre, post_gain.reshape(1, D))
    resid_all = resid.reshape(512, D)
    preact = jnp.dot(resid_all, enc_weight, preferred_element_type=f32) + enc_bias
    latents = jnp.maximum(preact, 0.0)
    latents_b = latents.astype(bf16)
    row_norms = jnp.sqrt(jnp.sum(jnp.square(dec_weight.astype(f32)), axis=1) + EPSILON)
    penalty = SPARSITY * jnp.sum((latents * row_norms).reshape(64, 8, 2, 128), axis=(0, 2))
    recon = jnp.dot(latents_b, dec_weight, preferred_element_type=f32).astype(bf16)
    error, stats = exchange_error(recon.reshape(BLOCKS, 8, D), resid, dec_bias.reshape(1, D), penalty)
    loss = jnp.sum(stats) / (512 * D)
    error_all = error.reshape(512, D)
    dec_bias_grad = jnp.sum(error_all, axis=0, dtype=f32)
    usage = jnp.sum(latents, axis=0)
    dec_grad = lax.dot_general(latents_b, error_all, (((0,), (0,)), ((), ())), preferred_element_type=f32)
    dec_grad = (dec_grad + SPARSITY * (usage / row_norms)[:, None] * dec_weight.astype(f32)).astype(bf16)
    latent_grad = lax.dot_general(error_all, dec_weight, (((1,), (1,)), ((), ())), preferred_element_type=f32)
    latent_grad = latent_grad + SPARSITY * row_norms
    preact_grad = latent_grad * jax.nn.sigmoid(preact / SMOOTHING)
    enc_bias_grad = jnp.sum(preact_grad, axis=0)
    enc_grad = lax.dot_general(
        resid_all, preact_grad.astype(bf16), (((0,), (0,)), ((), ())), preferred_element_type=f32
    ).astype(bf16)
    return (enc_grad, enc_bias_grad, dec_grad, dec_bias_grad, loss)


def solution(mesh):
    placed = (
        P("dp", "fsdp"),
        P("fsdp", None),
        P(("dp", "fsdp"), None),
        P(),
        P(None, ("dp", "fsdp")),
        P(("dp", "fsdp")),
        P(("dp", "fsdp"), None),
        P(),
    )
    return jax.shard_map(
        body,
        mesh=mesh,
        in_specs=placed,
        out_specs=(P(None, ("dp", "fsdp")), P(("dp", "fsdp")), P(("dp", "fsdp"), None), P(), P()),
        check_vma=False,
    )
```
